32 devices in a mesh: wide: 8 (over z, x), narrow: 4 (over y, core).
Axes of the slice: x: 2, y: 2, z: 4, core: 2. Of those that a mesh axis runs over, the one named last changes fastest.
Arguments:
- tokens: bfloat16 [384, 2560], P(('wide', 'narrow')), may hold values from -6 to 6
- scores: float32 [384], P(('wide', 'narrow')), may hold values from 0.25 to 1
- expert_ids: int32 [384], P(('wide', 'narrow')), may hold values from 0 to 15, as said below
- gate_halves: bfloat16 [32, 2560, 2048], P(('wide', 'narrow')), may hold values from -0.125 to 0.125
- up_halves: bfloat16 [32, 2560, 2048], P(('wide', 'narrow')), may hold values from -0.125 to 0.125
- shared_gate: bfloat16 [2560, 4096], P(None, 'narrow'), may hold values from -0.125 to 0.125
- shared_up: bfloat16 [2560, 4096], P(None, 'narrow'), may hold values from -0.125 to 0.125
Outputs:
- routed_hidden: bfloat16 [384, 4096], P(('wide', 'narrow'))
- shared_hidden: bfloat16 [384, 4096], P('wide', 'narrow')
The draws below stay inside these ranges and needn't reach their ends.
Inputs may be any that keep to these rules, and one draw needn't show every extreme that they name: `expert_ids`: within the 12 rows of each device no expert is named more than 2 times, and one expert, the same for every device, is named exactly 2 times in the rows of every device.
All inputs are finite; a program needn't handle non-finite values.
Results may differ from the reference program's by a relative error of at most 0.0058.
Values may be sent and summed in bfloat16 or wider, within the bound.
A program may use at most 128 MiB of HBM per device.

```python
import jax
import jax.numpy as jnp
from jax import lax

D = 2560
FE = 4096
FS = 4096
CAP = 2
EXPERTS = 16
ROWS_DEV = 12
TOKENS = 384
DEVICES = 32


def draw_expert_ids(key, part):
    hot_key, rest_key = jax.random.split(jax.random.fold_in(key, 11))
    hot_expert = jax.random.randint(hot_key, (), 0, EXPERTS).astype(jnp.int32)
    block_keys = jax.random.split(rest_key, TOKENS // ROWS_DEV)

    def one_block(block_key):
        pick_key, place_key = jax.random.split(block_key)
        shuffled = jax.random.permutation(pick_key, (EXPERTS - 1) * CAP)
        others = (shuffled[:ROWS_DEV - CAP] // CAP).astype(jnp.int32)
        others = others + (others >= hot_expert).astype(jnp.int32)
        chosen = jnp.concatenate([jnp.full((CAP,), hot_expert, jnp.int32), others])
        return jax.random.permutation(place_key, chosen)
    return jax.vmap(one_block)(block_keys).reshape(TOKENS).astype(jnp.int32)


def level_of(own_key, extent, shards, least, largest):
    gain = 1.0
    for axis_at, shards_of in shards:
        steps = jax.random.uniform(jax.random.fold_in(jax.random.fold_in(own_key, 6), axis_at), (shards_of,), jnp.float32, least / len(shards), largest / len(shards))
        gain = gain * jnp.repeat(jnp.exp(steps), extent[axis_at] // shards_of).reshape((-1,) + (1,) * (len(extent) - 1 - axis_at))
    return gain


def scatter_about(own_key, dims, width, bound, cuts=(), kind=jnp.bfloat16):
    result = jax.random.normal(own_key, dims, jnp.float32) * width
    if len(cuts) > 0:
        result = level_of(own_key, dims, cuts, -0.22, 0.18) * result
    return jnp.clip(result, min=-bound, max=bound).astype(kind)


def setup_inputs(seed: int = 0) -> dict:
    streams_of = jax.random.split(jax.random.key(seed), 8)
    tokens = scatter_about(streams_of[0], (TOKENS, D), 1.0, 6.0, ((0, 32),))
    scores = jnp.clip(0.25 + 0.75 * jax.random.uniform(streams_of[1], (TOKENS,), jnp.float32) ** level_of(streams_of[1], (TOKENS,), ((0, 32),), -0.2, 0.2), 0.25, 1.0)
    expert_ids = draw_expert_ids(jax.random.fold_in(streams_of[7], 71), 0)
    gate_halves = scatter_about(streams_of[3], (2 * EXPERTS, D, FE // 2), D ** -0.5, 0.125, ((0, 32),))
    up_halves = scatter_about(streams_of[4], (2 * EXPERTS, D, FE // 2), D ** -0.5, 0.125, ((0, 32),))
    shared_gate = scatter_about(streams_of[5], (D, FS), D ** -0.5, 0.125, ((1, 4),))
    shared_up = scatter_about(streams_of[6], (D, FS), D ** -0.5, 0.125, ((1, 4),))
    return {"tokens": tokens, "scores": scores, "expert_ids": expert_ids, "gate_halves": gate_halves, "up_halves": up_halves, "shared_gate": shared_gate, "shared_up": shared_up}


def swiglu_rows(inputs, gate_matrix, up_matrix):
    gate_val = jnp.dot(inputs, gate_matrix, preferred_element_type=jnp.float32)
    up_val = jnp.dot(inputs, up_matrix, preferred_element_type=jnp.float32)
    return (jax.nn.silu(gate_val) * up_val).astype(jnp.bfloat16)


def reference(tokens, scores, expert_ids, gate_halves, up_halves, shared_gate, shared_up):
    scaled = (tokens.astype(jnp.float32) * scores[:, None]).astype(jnp.bfloat16)
    capacity = CAP * DEVICES

    def one_expert(expert):
        members = jnp.nonzero(expert_ids == expert, size=capacity, fill_value=TOKENS)[0]
        picked = jnp.take(scaled, members, axis=0, mode="clip")
        gate_full = jnp.concatenate([gate_halves[2 * expert], gate_halves[2 * expert + 1]], axis=1)
        up_full = jnp.concatenate([up_halves[2 * expert], up_halves[2 * expert + 1]], axis=1)
        return swiglu_rows(picked, gate_full, up_full), members

    hidden, members = lax.map(one_expert, jnp.arange(EXPERTS, dtype=jnp.int32))
    routed = jnp.zeros((TOKENS, FE), jnp.bfloat16)
    routed = routed.at[members.reshape(-1)].set(hidden.reshape(-1, FE), mode="drop")
    shared = swiglu_rows(tokens, shared_gate, shared_up)
    return routed, shared
```

```python
import functools

import jax
import jax.numpy as jnp
from jax import lax
from jax.experimental import pallas as pl
from jax.experimental.pallas import tpu as pltpu
from jax.sharding import PartitionSpec as P

CAP = 2
CHUNKS = 2
UNROLL = True
TILE = 512
LIMIT = 44 * 1024 * 1024
MESH = pl.DeviceIdType.MESH


def silu_mul(gate_val, up_val):
    return (gate_val / (1.0 + jnp.exp(-gate_val))) * up_val


def kernel(
    wide, narrow,
    tokens_in, scores_in, ids_in, gate_ref, up_ref, sgate_ref, sup_ref,
    routed_ref, shared_ref,
    tokens_ref, scores_ref, ids_ref, wg, wu, sg, su, tok_all, outgoing, incoming, rows_x, sending, returned, flat,
    input_sem, weight_sem, tok_send, tok_recv, out_send, out_recv, pair_send, pair_recv, back_send, back_recv,
):
    devices = wide * narrow
    my_w = lax.axis_index("wide")
    my_n = lax.axis_index("narrow")
    me = my_w * narrow + my_n
    input_copies = [
        pltpu.make_async_copy(tokens_in, tokens_ref, input_sem.at[0]),
        pltpu.make_async_copy(scores_in, scores_ref, input_sem.at[1]),
        pltpu.make_async_copy(ids_in, ids_ref, input_sem.at[2]),
    ]
    for copy in input_copies:
        copy.start()
    rows, width = tokens_ref.shape
    padded = tok_all.shape[0] // narrow
    half_units = gate_ref.shape[2]
    experts = devices // 2
    part = half_units // CHUNKS
    shared_units = sgate_ref.shape[1]

    def dev(p):
        return (lax.div(p, narrow), lax.rem(p, narrow))

    barrier = pltpu.get_barrier_semaphore()

    def greet(k, carry):
        pl.semaphore_signal(barrier, inc=1, device_id=dev(lax.rem(me + k, devices)), device_id_type=MESH)
        return carry

    lax.fori_loop(1, devices, greet, 0, unroll=UNROLL)

    weight_copies = [
        pltpu.make_async_copy(sgate_ref, sg, weight_sem.at[0]),
        pltpu.make_async_copy(sup_ref, su, weight_sem.at[1]),
    ]
    for j in range(CHUNKS):
        cols = pl.ds(j * part, part)
        weight_copies.append(
            pltpu.make_async_copy(gate_ref.at[0, :, cols], wg.at[:, cols], weight_sem.at[2 + 2 * j])
        )
        weight_copies.append(
            pltpu.make_async_copy(up_ref.at[0, :, cols], wu.at[:, cols], weight_sem.at[3 + 2 * j])
        )
    for copy in weight_copies:
        copy.start()

    for copy in input_copies:
        copy.wait()
    tok = tokens_ref[...]
    ids_lane = ids_ref[...]
    r_sub = lax.broadcasted_iota(jnp.int32, (rows, rows), 0)
    r_lane = lax.broadcasted_iota(jnp.int32, (rows, rows), 1)
    eye = r_sub == r_lane
    scores_col = jnp.sum(jnp.where(eye, scores_ref[...], 0.0), axis=1, keepdims=True)
    idsf_lane = ids_lane.astype(jnp.float32)
    ids_col = jnp.sum(jnp.where(eye, idsf_lane, 0.0), axis=1, keepdims=True)
    same = ids_col == idsf_lane
    rank_lane = jnp.sum(jnp.where(same & (r_sub < r_lane), 1.0, 0.0), axis=0, keepdims=True)
    rank_col = jnp.sum(jnp.where(same & (r_lane < r_sub), 1.0, 0.0), axis=1, keepdims=True)
    slot_lane = (idsf_lane * CAP + rank_lane).astype(jnp.int32)
    slot_col = (ids_col * CAP + rank_col).astype(jnp.int32)
    cells = experts * CAP
    place = jnp.where(
        lax.broadcasted_iota(jnp.int32, (cells, rows), 0) == slot_lane, 1.0, 0.0
    ).astype(jnp.bfloat16)
    pick = jnp.where(
        lax.broadcasted_iota(jnp.int32, (rows, cells), 1) == slot_col, 1.0, 0.0
    ).astype(jnp.bfloat16)
    scaled = (tok.astype(jnp.float32) * scores_col).astype(jnp.bfloat16)
    placed = jnp.dot(place, scaled, preferred_element_type=jnp.float32).astype(jnp.bfloat16)
    for e in range(experts):
        outgoing[e] = placed[CAP * e : CAP * e + CAP, :]
    my_tok = pl.ds(pl.multiple_of(my_n * padded, padded), padded)
    if padded > rows:
        tok_all[my_tok, :] = jnp.concatenate(
            [tok, jnp.zeros((padded - rows, width), jnp.bfloat16)], axis=0
        )
    else:
        tok_all[my_tok, :] = tok

    pl.semaphore_wait(barrier, devices - 1)

    chips = devices // 2
    my_chip = me // 2
    my_core = me % 2
    partner = dev(my_chip * 2 + 1 - my_core)
    lanes = narrow // 2
    my_lane = my_n // 2
    pair_n = my_lane * 2 + 1 - my_core

    def out_copy(k):
        chip = lax.rem(my_chip + k, chips)
        return pltpu.make_async_remote_copy(
            src_ref=outgoing.at[chip], dst_ref=incoming.at[my_core, my_chip],
            send_sem=out_send, recv_sem=out_recv,
            device_id=dev(chip * 2 + my_core), device_id_type=MESH,
        )

    def start_out(k, carry):
        out_copy(k).start()
        return carry

    lax.fori_loop(1, chips, start_out, 0, unroll=UNROLL)
    incoming[my_core, my_chip] = outgoing[my_chip]

    def tok_slab(n):
        return tok_all.at[pl.ds(pl.multiple_of(n * padded, padded), padded), :]

    def tok_copy(k, n):
        to = ((my_lane + k) % lanes) * 2 + my_core
        return pltpu.make_async_remote_copy(
            src_ref=tok_slab(n), dst_ref=tok_slab(n),
            send_sem=tok_send.at[k], recv_sem=tok_recv.at[k],
            device_id=(my_w, to), device_id_type=MESH,
        )

    def tok_pass(k, n):
        return pltpu.make_async_remote_copy(
            src_ref=tok_slab(n), dst_ref=tok_slab(n),
            send_sem=tok_send.at[lanes + k], recv_sem=tok_recv.at[lanes + k],
            device_id=(my_w, pair_n), device_id_type=MESH,
        )

    for k in range(1, lanes):
        tok_copy(k, my_n).start()
    tok_pass(0, my_n).start()

    others = pl.ds(0, chips - 1)
    all_out = pltpu.make_async_remote_copy(
        src_ref=outgoing.at[others], dst_ref=incoming.at[my_core, others],
        send_sem=out_send, recv_sem=out_recv,
        device_id=partner, device_id_type=MESH,
    )
    all_out.wait_recv()

    def pair_copy(core):
        return pltpu.make_async_remote_copy(
            src_ref=incoming.at[core], dst_ref=incoming.at[core],
            send_sem=pair_send, recv_sem=pair_recv,
            device_id=partner, device_id_type=MESH,
        )

    pair_copy(my_core).start()
    for k in range(1, lanes):
        origin = ((my_lane + lanes - k) % lanes) * 2 + my_core
        tok_copy(k, origin).wait_recv()
        tok_pass(k, origin).start()

    def fill_rows(core):
        first = pl.multiple_of(core * (chips * CAP), chips * CAP)
        half = rows_x.at[pl.ds(first, chips * CAP), :]
        for s in range(chips):
            half[CAP * s : CAP * s + CAP, :] = incoming[core, s]

    fill_rows(my_core)
    pair_copy(1 - my_core).wait_recv()
    fill_rows(1 - my_core)

    my_slot = my_core * chips + my_chip

    def back_copy(j, k):
        p = lax.rem(me + k, devices)
        return pltpu.make_async_remote_copy(
            src_ref=sending.at[j, lax.rem(p, 2) * chips + lax.div(p, 2)],
            dst_ref=returned.at[j, my_slot],
            send_sem=back_send.at[j], recv_sem=back_recv.at[j],
            device_id=dev(p), device_id_type=MESH,
        )

    def all_back(j):
        rest = pl.ds(0, devices - 1)
        return pltpu.make_async_remote_copy(
            src_ref=sending.at[j, rest], dst_ref=returned.at[j, rest],
            send_sem=back_send.at[j], recv_sem=back_recv.at[j],
            device_id=partner, device_id_type=MESH,
        )

    step_cols = min(TILE, part)
    for j in range(CHUNKS):
        weight_copies[2 + 2 * j].wait()
        weight_copies[3 + 2 * j].wait()

        def routed_step(i, carry):
            at = pl.multiple_of(j * part + i * step_cols, step_cols)
            cols = pl.ds(at, step_cols)
            gate_val = jnp.dot(rows_x[...], wg[:, cols], preferred_element_type=jnp.float32)
            up_val = jnp.dot(rows_x[...], wu[:, cols], preferred_element_type=jnp.float32)
            hidden = silu_mul(gate_val, up_val).astype(jnp.bfloat16)
            local = pl.ds(pl.multiple_of(i * step_cols, step_cols), step_cols)
            for s in range(devices):
                at_row = CAP * s
                sending[j, s, :, local] = hidden[at_row : at_row + CAP, :]
            return carry

        lax.fori_loop(0, part // step_cols, routed_step, 0)

        def start_back(k, carry):
            back_copy(j, k).start()
            return carry

        lax.fori_loop(1, devices, start_back, 0, unroll=UNROLL)
        returned[j, my_slot] = sending[j, my_slot]

    for k in range(lanes):
        origin = ((my_lane + lanes - k) % lanes) * 2 + 1 - my_core
        tok_pass(k, origin).wait_recv()
    weight_copies[0].wait()
    weight_copies[1].wait()

    tile = min(TILE, shared_units)

    def shared_step(i, carry):
        cols = pl.ds(pl.multiple_of(i * tile, tile), tile)
        gate_val = jnp.dot(tok_all[...], sg[:, cols], preferred_element_type=jnp.float32)
        up_val = jnp.dot(tok_all[...], su[:, cols], preferred_element_type=jnp.float32)
        hidden = silu_mul(gate_val, up_val)
        packed = jnp.concatenate(
            [hidden[n * padded : n * padded + rows, :] for n in range(narrow)], axis=0
        )
        shared_ref[:, cols] = packed.astype(jnp.bfloat16)
        return carry

    lax.fori_loop(0, shared_units // tile, shared_step, 0)

    for j in range(CHUNKS):
        all_back(j).wait_recv()
        for h in range(2):
            for e in range(experts):
                flat[CAP * e : CAP * e + CAP, :] = returned[j, h * experts + e]
            got = jnp.dot(pick, flat[...], preferred_element_type=jnp.float32)
            start = h * half_units + j * part
            routed_ref[:, start : start + part] = got.astype(jnp.bfloat16)

    for k in range(1, lanes):
        tok_copy(k, my_n).wait_send()
    for k in range(lanes):
        tok_pass(k, my_n).wait_send()
    pair_copy(my_core).wait_send()

    all_out.wait_send()
    for j in range(CHUNKS):
        all_back(j).wait_send()


def hand_on(routed_in, shared_in, routed_out, shared_out, sem):
    copies = [
        pltpu.make_async_copy(routed_in, routed_out, sem.at[0]),
        pltpu.make_async_copy(shared_in, shared_out, sem.at[1]),
    ]
    for copy in copies:
        copy.start()
    for copy in copies:
        copy.wait()


def shards(wide, narrow, tokens, scores, expert_ids, gate_halves, up_halves, shared_gate, shared_up):
    devices = wide * narrow
    rows, width = tokens.shape
    half_units = gate_halves.shape[2]
    shared_units = shared_gate.shape[1]
    padded = -(-rows // 16) * 16
    part = half_units // CHUNKS
    bf16 = jnp.bfloat16
    vmem = pl.BlockSpec(memory_space=pltpu.VMEM)
    hbm = pl.BlockSpec(memory_space=pl.ANY)
    dma = pltpu.SemaphoreType.DMA
    outs = pl.pallas_call(
        functools.partial(kernel, wide, narrow),
        out_shape=(
            jax.ShapeDtypeStruct((rows, 2 * half_units), bf16),
            jax.ShapeDtypeStruct((rows * narrow, shared_units), bf16),
        ),
        in_specs=[hbm] * 7,
        out_specs=(vmem, vmem),
        scratch_shapes=[
            pltpu.VMEM((rows, width), bf16),
            pltpu.VMEM((1, rows), jnp.float32),
            pltpu.VMEM((1, rows), jnp.int32),
            pltpu.VMEM((width, half_units), bf16),
            pltpu.VMEM((width, half_units), bf16),
            pltpu.VMEM((width, shared_units), bf16),
            pltpu.VMEM((width, shared_units), bf16),
            pltpu.VMEM((narrow * padded, width), bf16),
            pltpu.VMEM((devices // 2, CAP, width), bf16),
            pltpu.VMEM((2, devices // 2, CAP, width), bf16),
            pltpu.VMEM((devices * CAP, width), bf16),
            pltpu.VMEM((CHUNKS, devices, CAP, part), bf16),
            pltpu.VMEM((CHUNKS, devices, CAP, part), bf16),
            pltpu.VMEM((devices // 2 * CAP, part), bf16),
            dma((3,)),
            dma((2 + 2 * CHUNKS,)),
            dma((narrow,)),
            dma((narrow,)),
            dma,
            dma,
            dma,
            dma,
            dma((CHUNKS,)),
            dma((CHUNKS,)),
        ],
        compiler_params=pltpu.CompilerParams(collective_id=0, has_side_effects=True, vmem_limit_bytes=LIMIT),
    )(*(
        pltpu.with_memory_space_constraint(a, pltpu.HBM)
        for a in (tokens, scores[None, :], expert_ids[None, :], gate_halves, up_halves, shared_gate, shared_up)
    ))
    return pl.pallas_call(
        hand_on,
        out_shape=tuple(jax.ShapeDtypeStruct(o.shape, o.dtype) for o in outs),
        in_specs=[vmem, vmem],
        out_specs=(hbm, hbm),
        scratch_shapes=[dma((2,))],
        compiler_params=pltpu.CompilerParams(vmem_limit_bytes=1024 * 1024),
    )(*outs)


def solution(mesh):
    placed = (
        P(("wide", "narrow"), None),
        P(("wide", "narrow")),
        P(("wide", "narrow")),
        P(("wide", "narrow"), None, None),
        P(("wide", "narrow"), None, None),
        P(None, "narrow"),
        P(None, "narrow"),
    )
    return jax.shard_map(
        functools.partial(shards, mesh.shape["wide"], mesh.shape["narrow"]),
        mesh=mesh,
        in_specs=placed,
        out_specs=(P(("wide", "narrow"), None), P("wide", "narrow")),
        check_vma=False,
    )
```
